256 devices in a mesh: sens: 64 (over z_hi, y, x, core), hour: 4 (over z_lo).
Axes of the slice: x: 4, y: 4, z: 8 (z_hi: 2, z_lo: 4; z = z_hi * 4 + z_lo), core: 2. Of those that a mesh axis runs over, the one named last changes fastest.
Arguments:
- sky: bfloat16 [512, 146], P('hour'), may hold values from 0.049804688 to 1
- sky_open: bfloat16 [146, 131072], P(None, 'sens'), may hold values from 0 to 0.013977051
- sky_closed: bfloat16 [146, 131072], P(None, 'sens'), may hold values from 0 to 0.0039978027
- sun_coef: bfloat16 [5165, 131072], P(None, ('sens', 'hour')), may hold values from 0 to 1
- sun_bins: int32 [512, 4], P('hour'), may hold values from 0 to 5164, as said below
- sun_rad: bfloat16 [512, 4], P('hour'), may hold values from 0.099609375 to 1
- target: bfloat16 [512, 131072], P('hour', 'sens'), may hold values from 0 to 2
- zone_of: int32 [65536, 1], P('sens'), may hold values from 0 to 63
- area: float32 [65536], P('sens'), may hold values from 0.5 to 4
- openness: float32 [65536], P('sens'), may hold values from 0 to 1
Outputs:
- illuminance: bfloat16 [512, 131072], P('hour', 'sens')
- new_openness: float32 [65536], P('sens')
The draws below stay inside these ranges and needn't reach their ends.
Inputs may be any that keep to these rules, and one draw needn't show every extreme that they name: `sun_bins`: the 4 bins of one hour are consecutive modulo 5165, hence distinct. `zone_of`: every zone has at least one window.
All inputs are finite; a program needn't handle non-finite values.
Results may differ from the reference program's by a relative error of at most 0.001.
Values may be sent and summed in bfloat16 or wider, within the bound.
A program may use at most 128 MiB of HBM per device.

```python
import math
import jax
import jax.numpy as jnp
from jax import lax

NBINS = 5165
PATCHES = 146
KBINS = 4
HOURS = 512
SENS_BLK = 2048
SENSORS = 131072
ZONES = 64
WIN = 65536


def draw_sun_bins(key, part):
    start = jax.random.randint(key, (HOURS,), 0, NBINS)
    start = start.at[0].set(NBINS - KBINS).at[1].set(0)
    return ((start[:, None] + jnp.arange(KBINS)[None, :]) % NBINS).astype(jnp.int32)


def block_levels(own_key, dims, shards, low, largest):
    def one(dim, shards_of):
        heights = jax.random.uniform(jax.random.fold_in(jax.random.fold_in(own_key, 6), dim), (shards_of,), jnp.float32, low / len(shards), largest / len(shards))
        return jnp.repeat(jnp.exp(heights), dims[dim] // shards_of).reshape((-1,) + (1,) * (len(dims) - dim - 1))

    factor_of = one(*shards[0])
    for cut in shards[1:]:
        factor_of = factor_of * one(*cut)
    return factor_of


def different_ones(key, rows, count, top, lift):
    ranking = jax.random.permutation(jax.random.fold_in(key, 1), count)
    favour = ranking
    for power in range(3):
        favour = favour * favour // count
    favour = favour * lift // count
    chance = jax.random.randint(jax.random.fold_in(key, 2), (rows, count), 0, 4096) + favour
    sure = jax.random.permutation(jax.random.fold_in(key, 3), rows)[jnp.arange(count) % rows]
    chance = jnp.where(jnp.arange(rows)[:, None] == sure[None, :], 1 << 14, chance)
    merit = chance * count + jnp.arange(count)
    return lax.top_k(merit.astype(jnp.int32), top)[1].astype(jnp.int32)


def setup_inputs(seed: int = 0) -> dict:
    keys = jax.random.split(jax.random.key(seed), 11)
    return {
        "sky": jnp.clip(jnp.exp(math.log(1.0) - 2.9996462 * jax.random.uniform(keys[0], (HOURS, PATCHES), jnp.float32) ** block_levels(keys[0], (HOURS, PATCHES), ((0, 4),), -0.2, 0.2)), 0.049804688, 1.0).astype(jnp.bfloat16),
        "sky_open": jnp.clip(0.013977051 * jax.random.uniform(keys[1], (PATCHES, SENSORS), jnp.float32) ** block_levels(keys[1], (PATCHES, SENSORS), ((1, 64),), -0.2, 0.2), 0.0, 0.013977051).astype(jnp.bfloat16),
        "sky_closed": jnp.clip(0.0039978027 * jax.random.uniform(keys[2], (PATCHES, SENSORS), jnp.float32) ** block_levels(keys[2], (PATCHES, SENSORS), ((1, 64),), -0.2, 0.2), 0.0, 0.0039978027).astype(jnp.bfloat16),
        "sun_coef": jnp.clip(1.0 * jax.random.uniform(keys[3], (NBINS, SENSORS), jnp.float32) ** block_levels(keys[3], (NBINS, SENSORS), ((1, 256),), -0.2, 0.2), 0.0, 1.0).astype(jnp.bfloat16),
        "sun_bins": draw_sun_bins(jax.random.fold_in(keys[10], 71), 0),
        "sun_rad": jnp.clip(jnp.exp(math.log(1.0) - 2.306499 * jax.random.uniform(keys[5], (HOURS, KBINS), jnp.float32) ** block_levels(keys[5], (HOURS, KBINS), ((0, 4),), -0.2, 0.2)), 0.099609375, 1.0).astype(jnp.bfloat16),
        "target": jnp.clip(2.0 * jax.random.uniform(keys[6], (HOURS, SENSORS), jnp.float32) ** block_levels(keys[6], (HOURS, SENSORS), ((0, 4), (1, 64)), -0.2, 0.2), 0.0, 2.0).astype(jnp.bfloat16),
        "zone_of": different_ones(keys[7], WIN, ZONES, 1, 256),
        "area": jnp.clip(jnp.exp(math.log(4.0) - 2.0794415 * jax.random.uniform(keys[8], (WIN,), jnp.float32) ** block_levels(keys[8], (WIN,), ((0, 64),), -0.2, 0.2)), 0.5, 4.0),
        "openness": jnp.clip(1.0 * jax.random.uniform(keys[9], (WIN,), jnp.float32) ** block_levels(keys[9], (WIN,), ((0, 64),), -0.2, 0.2), 0.0, 1.0),
    }


def reference(sky, sky_open, sky_closed, sun_coef, sun_bins, sun_rad, target, zone_of, area, openness):
    member = (zone_of[:, 0][:, None] == jnp.arange(ZONES, dtype=jnp.int32)[None, :]).astype(jnp.float32)
    stacked = jnp.stack([area * openness, area, area * area])
    sums = jnp.dot(stacked, member, precision=lax.Precision.HIGHEST)
    share = sums[0] / sums[1]
    op_part = jnp.dot(sky, sky_open, preferred_element_type=jnp.float32)
    cl_part = jnp.dot(sky, sky_closed, preferred_element_type=jnp.float32)
    picked = jnp.take(sun_coef, sun_bins.reshape(-1), axis=0).reshape(HOURS, KBINS, SENSORS)
    sun_part = jnp.einsum('hk,hks->hs', sun_rad.astype(jnp.float32), picked.astype(jnp.float32))
    cross = op_part - cl_part + sun_part
    share_s = jnp.repeat(share, SENS_BLK)
    lit = cl_part + share_s[None, :] * cross
    terms = lax.optimization_barrier(jnp.sum(2.0 * (lit - target.astype(jnp.float32)) * cross, axis=0))
    zone_grad = lax.optimization_barrier(jnp.sum(terms.reshape(ZONES, SENS_BLK), axis=1))
    ratio = zone_grad / sums[1]
    grad = area * jnp.dot(member, ratio, precision=lax.Precision.HIGHEST)
    rms = jnp.sqrt(jnp.sum(grad * grad) / WIN + 1e-06)
    new_openness = jnp.clip(openness - 0.25 * grad / rms, 0.0, 1.0)
    return (lit.astype(jnp.bfloat16), new_openness)
```

```python
import functools

import jax
import jax.numpy as jnp
from jax import lax
from jax.experimental import pallas as pl
from jax.experimental.pallas import tpu as pltpu
from jax.sharding import PartitionSpec as P

MESH = pl.DeviceIdType.MESH
F32 = jnp.float32
BF16 = jnp.bfloat16
HIGH = lax.Precision.HIGHEST
SIDE = 8
LANES = 128
ROWS = 32


def kernel(
    hours,
    windows_all,
    sky_hbm,
    open_hbm,
    closed_hbm,
    coef_hbm,
    bins_ref,
    rad_ref,
    target_hbm,
    zone_ref,
    area_ref,
    openness_ref,
    lit_hbm,
    new_ref,
    coef,
    tail_wide,
    tail,
    weights,
    columns,
    bins,
    sky,
    target,
    open_own,
    closed_own,
    cross,
    lit,
    lit_out,
    member,
    stat_a,
    stat_b,
    grad_h,
    grad_a,
    grad_b,
    local_sem,
    hour_send,
    hour_recv,
    side_send,
    side_recv,
):
    s = lax.axis_index("sens")
    h = lax.axis_index("hour")
    low = lax.rem(s, SIDE)
    high = s // SIDE
    nbins, own = coef.shape
    block = sky.shape[2]
    whole = nbins // LANES * LANES
    zones = zone_ref.shape[1] * 0 + SIDE * SIDE

    def hour_of(d):
        return (s, lax.rem(h + d, hours))

    def back_of(d):
        return (s, lax.rem(h + hours - d, hours))

    def low_of(d):
        return (high * SIDE + lax.rem(low + d, SIDE), h)

    def high_of(d):
        return (lax.rem(high + d, SIDE) * SIDE + low, h)

    barrier = pltpu.get_barrier_semaphore()
    for d in range(1, hours):
        pl.semaphore_signal(barrier, inc=1, device_id=hour_of(d), device_id_type=MESH)
    for d in range(1, SIDE):
        pl.semaphore_signal(barrier, inc=1, device_id=low_of(d), device_id_type=MESH)
        pl.semaphore_signal(barrier, inc=1, device_id=high_of(d), device_id_type=MESH)

    own_columns = pl.ds(pl.multiple_of(h * own, own), own)
    chunk = 1024
    local = []
    for at in range(0, nbins, chunk):
        rows = pl.ds(at, min(chunk, nbins - at))
        local.append(pltpu.make_async_copy(coef_hbm.at[rows], coef.at[rows], local_sem.at[len(local)]))
    local.append(pltpu.make_async_copy(open_hbm.at[:, own_columns], open_own, local_sem.at[len(local)]))
    local.append(pltpu.make_async_copy(closed_hbm.at[:, own_columns], closed_own, local_sem.at[len(local)]))
    local.append(pltpu.make_async_copy(target_hbm.at[:, own_columns], target.at[0], local_sem.at[len(local)]))
    sky_copy = pltpu.make_async_copy(sky_hbm, sky.at[0], local_sem.at[len(local)])
    local.append(sky_copy)
    for copy in local:
        copy.start()

    bins[0, 0:4, :] = bins_ref[...].astype(F32)
    bins[0, 4:8, :] = rad_ref[...].astype(F32)

    area = area_ref[...]
    row = lax.broadcasted_iota(jnp.int32, (SIDE, area.shape[1]), 0)
    zone_row = lax.broadcasted_iota(jnp.int32, member.shape, 0)
    member[...] = jnp.where(zone_row == zone_ref[...], 1.0, 0.0).astype(F32)
    stacked = jnp.where(
        row == 0, area * openness_ref[...], jnp.where(row == 1, area, jnp.where(row == 2, area * area, 0.0))
    )
    stat_a[0] = lax.dot_general(
        stacked, member[...], (((1,), (1,)), ((), ())), precision=HIGH, preferred_element_type=F32
    )

    pl.semaphore_wait(barrier, hours - 1 + 2 * (SIDE - 1))

    def to_hour(source, target_of, d, kind, device):
        return pltpu.make_async_remote_copy(
            src_ref=source,
            dst_ref=target_of,
            send_sem=hour_send.at[kind, d],
            recv_sem=hour_recv.at[kind, d],
            device_id=device,
            device_id_type=MESH,
        )

    def to_side(buffer, d, kind, device):
        return pltpu.make_async_remote_copy(
            src_ref=buffer.at[0],
            dst_ref=buffer.at[d],
            send_sem=side_send.at[kind, d],
            recv_sem=side_recv.at[kind, d],
            device_id=device,
            device_id_type=MESH,
        )

    bins_copies = [to_hour(bins.at[0], bins.at[d], d, 0, hour_of(d)) for d in range(1, hours)]
    for copy in bins_copies:
        copy.start()
    stat_a_copies = [to_side(stat_a, d, 0, low_of(d)) for d in range(1, SIDE)]
    for copy in stat_a_copies:
        copy.start()
    sky_copies = [to_hour(sky_hbm, sky.at[d], d, 1, hour_of(d)) for d in range(1, hours)]
    for copy in sky_copies:
        copy.start()
    target_copies = []
    for d in range(1, hours):
        there = lax.rem(h + d, hours)
        place = pl.ds(pl.multiple_of(there * own, own), own)
        target_copies.append(to_hour(target_hbm.at[:, place], target.at[d], d, 2, hour_of(d)))
    for copy in target_copies:
        copy.start()

    lane = lax.broadcasted_iota(jnp.int32, (ROWS, LANES), 1).astype(F32)

    def build(d):
        columns[d * block : (d + 1) * block, :] = bins[d].T

        def rows_of(r, carry):
            at = pl.multiple_of(d * block + r * ROWS, ROWS)
            mine = columns[pl.ds(at, ROWS), :]
            place = [jnp.broadcast_to(mine[:, k : k + 1], (ROWS, LANES)) - lane for k in range(4)]
            value = [jnp.broadcast_to(mine[:, 4 + k : 5 + k], (ROWS, LANES)) for k in range(4)]
            for c in range(weights.shape[1] // LANES):
                first = float(c * LANES)
                w = jnp.zeros((ROWS, LANES), F32)
                for k in range(4):
                    w = jnp.where(place[k] == first, value[k], w)
                weights[pl.ds(at, ROWS), c * LANES : (c + 1) * LANES] = w.astype(BF16)
            return carry

        lax.fori_loop(0, block // ROWS, rows_of, 0)

    build(0)

    def total_of(buffer, me, count):
        total = buffer[lax.rem(me, count)]
        for m in range(1, count):
            total = total + buffer[lax.rem(me + count - m, count)]
        return total

    for copy in stat_a_copies:
        copy.wait_recv()
    stat_b[0] = total_of(stat_a, low, SIDE)
    stat_b_copies = [to_side(stat_b, d, 1, high_of(d)) for d in range(1, SIDE)]
    for copy in stat_b_copies:
        copy.start()

    for d in range(1, hours):
        bins_copies[d - 1].wait_recv()
        build(d)
    for copy in local:
        copy.wait()

    tail_wide[...] = jnp.zeros_like(tail_wide)
    tail_wide[0 : nbins - whole, :] = coef[whole:nbins, :].astype(F32)
    tail[...] = tail_wide[...].astype(BF16)

    for copy in stat_b_copies:
        copy.wait_recv()
    sums = total_of(stat_b, high, SIDE)
    zone_lane = lax.broadcasted_iota(jnp.int32, (1, LANES), 1)
    den = jnp.where(zone_lane < zones, sums[1:2], 1.0)
    shares = sums[0:1] / den
    share = jnp.sum(jnp.where(zone_lane == s, shares, 0.0), axis=1, keepdims=True)

    lit_copies = []
    for d in (1, 2, 3, 0):
        if d:
            sky_copies[d - 1].wait_recv()
        here = pl.ds(d * block, block)
        first = (((0,), (0,)), ((), ()))
        op_part = lax.dot_general(sky[d], open_own[...], first, preferred_element_type=F32)
        cl_part = lax.dot_general(sky[d], closed_own[...], first, preferred_element_type=F32)
        sun = jnp.dot(weights[here, 0:whole], coef[0:whole, :], preferred_element_type=F32)
        sun = sun + jnp.dot(weights[here, whole:], tail[...], preferred_element_type=F32)
        both = op_part - cl_part + sun
        cross[d] = both
        level = cl_part + share * both
        lit[d] = level
        lit_out[d] = level.astype(BF16)
        if d:
            copy = to_hour(lit_out.at[d], lit_hbm.at[:, own_columns], d, 3, back_of(d))
            copy.start()
            lit_copies.append(copy)
    own_out = pltpu.make_async_copy(lit_out.at[0], lit_hbm.at[:, own_columns], local_sem.at[0])
    own_out.start()

    terms = jnp.zeros((1, own), F32)
    for d in range(hours):
        if d:
            target_copies[d - 1].wait_recv()
        part = 2.0 * (lit[d] - target[d].astype(F32)) * cross[d]
        terms = terms + jnp.sum(part, axis=0, keepdims=True)
    local_grad = jnp.sum(terms, axis=1, keepdims=True)
    tile_lane = lax.broadcasted_iota(jnp.int32, (SIDE, LANES), 1)
    grad_h[0] = jnp.where(tile_lane == s, local_grad, 0.0)
    copies_h = [to_hour(grad_h.at[0], grad_h.at[d], d, 4, hour_of(d)) for d in range(1, hours)]
    for copy in copies_h:
        copy.start()
    for copy in copies_h:
        copy.wait_recv()
    grad_a[0] = total_of(grad_h, h, hours)
    copies_a = [to_side(grad_a, d, 2, low_of(d)) for d in range(1, SIDE)]
    for copy in copies_a:
        copy.start()
    for copy in copies_a:
        copy.wait_recv()
    grad_b[0] = total_of(grad_a, low, SIDE)
    copies_b = [to_side(grad_b, d, 3, high_of(d)) for d in range(1, SIDE)]
    for copy in copies_b:
        copy.start()
    for copy in copies_b:
        copy.wait_recv()
    zone_grad = total_of(grad_b, high, SIDE)
    ratio = zone_grad / den
    square = jnp.sum(ratio[0:1] * ratio[0:1] * sums[2:3], axis=1, keepdims=True)
    rms = jnp.sqrt(square / windows_all + 1e-06)
    spread = jnp.dot(ratio, member[...], precision=HIGH, preferred_element_type=F32)
    grad = area * spread[0:1]
    new_ref[...] = jnp.clip(openness_ref[...] - 0.25 * grad / rms, 0.0, 1.0)

    for copy in bins_copies + sky_copies + target_copies + copies_h:
        copy.wait_send()
    for copy in stat_a_copies + stat_b_copies + copies_a + copies_b:
        copy.wait_send()
    own_out.wait()
    for copy in lit_copies:
        copy.wait()


def solution(mesh):
    hours = mesh.shape["hour"]
    sens = mesh.shape["sens"]

    def step(sky, sky_open, sky_closed, sun_coef, sun_bins, sun_rad, target, zone_of, area, openness):
        block, patches = sky.shape
        nbins, own = sun_coef.shape
        windows = area.shape[0]
        padded = pl.cdiv(nbins, LANES) * LANES
        any_space = pl.BlockSpec(memory_space=pl.ANY)
        vmem = pl.BlockSpec(memory_space=pltpu.VMEM)
        tile = (SIDE, LANES)
        lit, new = pl.pallas_call(
            functools.partial(kernel, hours, windows * sens),
            out_shape=(
                jax.ShapeDtypeStruct((block, own * hours), BF16),
                jax.ShapeDtypeStruct((1, windows), F32),
            ),
            in_specs=[any_space, any_space, any_space, any_space, vmem, vmem, any_space, vmem, vmem, vmem],
            out_specs=(any_space, vmem),
            scratch_shapes=[
                pltpu.VMEM((nbins, own), BF16),
                pltpu.VMEM((LANES, own), F32),
                pltpu.VMEM((LANES, own), BF16),
                pltpu.VMEM((hours * block, padded), BF16),
                pltpu.VMEM((hours * block, SIDE), F32),
                pltpu.VMEM((hours,) + tile, F32),
                pltpu.VMEM((hours, patches, block), BF16),
                pltpu.VMEM((hours, block, own), BF16),
                pltpu.VMEM((patches, own), BF16),
                pltpu.VMEM((patches, own), BF16),
                pltpu.VMEM((hours, block, own), F32),
                pltpu.VMEM((hours, block, own), F32),
                pltpu.VMEM((hours, block, own), BF16),
                pltpu.VMEM((LANES, windows), F32),
                pltpu.VMEM((SIDE,) + tile, F32),
                pltpu.VMEM((SIDE,) + tile, F32),
                pltpu.VMEM((hours,) + tile, F32),
                pltpu.VMEM((SIDE,) + tile, F32),
                pltpu.VMEM((SIDE,) + tile, F32),
                pltpu.SemaphoreType.DMA((16,)),
                pltpu.SemaphoreType.DMA((5, hours)),
                pltpu.SemaphoreType.DMA((5, hours)),
                pltpu.SemaphoreType.DMA((4, SIDE)),
                pltpu.SemaphoreType.DMA((4, SIDE)),
            ],
            compiler_params=pltpu.CompilerParams(
                collective_id=0, has_side_effects=True, vmem_limit_bytes=48 << 20
            ),
        )(
            sky.T,
            sky_open,
            sky_closed,
            sun_coef,
            sun_bins.T,
            sun_rad.T,
            target,
            zone_of.T,
            area[None, :],
            openness[None, :],
        )
        return lit, new[0]

    in_specs = (
        P("hour", None),
        P(None, "sens"),
        P(None, "sens"),
        P(None, ("sens", "hour")),
        P("hour", None),
        P("hour", None),
        P("hour", "sens"),
        P("sens", None),
        P("sens"),
        P("sens"),
    )
    out_specs = (P("hour", "sens"), P("sens"))
    return jax.shard_map(step, mesh=mesh, in_specs=in_specs, out_specs=out_specs, check_vma=False)
```

```python
import functools

import jax
import jax.numpy as jnp
from jax import lax
from jax.experimental import pallas as pl
from jax.experimental.pallas import tpu as pltpu
from jax.sharding import PartitionSpec as P

MESH = pl.DeviceIdType.MESH
F32 = jnp.float32
BF16 = jnp.bfloat16
HIGH = lax.Precision.HIGHEST
SIDE = 8
YS = 4
PLANE = SIDE * YS
PIECE = 24
LANES = 128
ROWS = 32


def kernel(
    hours,
    windows_all,
    sky_hbm,
    open_hbm,
    closed_hbm,
    coef_hbm,
    bins_hbm,
    rad_hbm,
    target_hbm,
    zone_hbm,
    area_hbm,
    openness_hbm,
    lit_hbm,
    new_ref,
    bins_ref,
    rad_ref,
    zone_ref,
    area_ref,
    openness_ref,
    coef,
    tail_wide,
    tail,
    weights,
    columns,
    bins,
    sky_in,
    sky,
    target,
    open_own,
    closed_own,
    cross,
    lit,
    lit_out,
    member,
    stat_low,
    stat_y,
    stat_half,
    grad_z,
    grad_plane,
    local_sem,
    hour_send,
    hour_recv,
    low_send,
    low_recv,
    y_send,
    y_recv,
    half_send,
    half_recv,
    z_send,
    z_recv,
    plane_send,
    plane_recv,
):
    s = lax.axis_index("sens")
    h = lax.axis_index("hour")
    low = lax.rem(s, SIDE)
    y = lax.rem(s // SIDE, YS)
    plane = lax.rem(s, PLANE)
    half = s // PLANE
    z = half * hours + h
    zs = 2 * hours
    nbins, own = coef.shape
    block = sky.shape[2]
    patches = sky_in.shape[0]
    whole = nbins // LANES * LANES

    def hour_of(d):
        return (s, lax.rem(h + d, hours))

    def low_of(d):
        return (s - low + lax.rem(low + d, SIDE), h)

    def y_of(d):
        return (half * PLANE + lax.rem(y + d, YS) * SIDE + low, h)

    def plane_of(d):
        return (half * PLANE + lax.rem(plane + d, PLANE), h)

    def z_of(d):
        there = lax.rem(z + d, zs)
        return (there // hours * PLANE + plane, lax.rem(there, hours))

    giver = ((1 - half) * PLANE + plane, (hours - 1) * (1 - h // 2))
    at_end = lax.rem(h, hours - 1) == 0
    first_taker = (hours - 1 - h) // (hours - 1) * 2

    def taker(t):
        return ((1 - half) * PLANE + plane, first_taker + t)

    barrier = pltpu.get_barrier_semaphore()
    for d in range(1, hours):
        pl.semaphore_signal(barrier, inc=1, device_id=hour_of(d), device_id_type=MESH)
    pl.semaphore_signal(barrier, inc=1, device_id=giver, device_id_type=MESH)
    for d in range(1, SIDE):
        pl.semaphore_signal(barrier, inc=1, device_id=low_of(d), device_id_type=MESH)
    for d in range(1, YS):
        pl.semaphore_signal(barrier, inc=1, device_id=y_of(d), device_id_type=MESH)

    own_columns = pl.ds(pl.multiple_of(h * own, own), own)
    small = []
    for source, held in (
        (bins_hbm, bins_ref),
        (rad_hbm, rad_ref),
        (sky_hbm, sky_in),
        (zone_hbm, zone_ref),
        (area_hbm, area_ref),
        (openness_hbm, openness_ref),
    ):
        small.append(pltpu.make_async_copy(source, held, local_sem.at[len(small)]))
    local = []
    chunk = 1024
    for at in range(0, nbins, chunk):
        rows = pl.ds(at, min(chunk, nbins - at))
        local.append((coef_hbm.at[rows], coef.at[rows]))
    local.append((open_hbm.at[:, own_columns], open_own))
    local.append((closed_hbm.at[:, own_columns], closed_own))
    local.append((target_hbm.at[:, own_columns], target.at[0]))
    local = [
        pltpu.make_async_copy(source, held, local_sem.at[len(small) + i]) for i, (source, held) in enumerate(local)
    ]
    for copy in small + local:
        copy.start()
    for copy in small:
        copy.wait()

    bins[0, 0:4, :] = bins_ref[...].astype(F32)
    bins[0, 4:8, :] = rad_ref[...].astype(F32)
    sky[0, patches // 16 * 16 :, :] = jnp.zeros_like(sky[0, patches // 16 * 16 :, :])
    sky[0, 0:patches, :] = sky_in[...]

    area = area_ref[...]
    row = lax.broadcasted_iota(jnp.int32, (SIDE, area.shape[1]), 0)
    zone_row = lax.broadcasted_iota(jnp.int32, member.shape, 0)
    member[...] = jnp.where(zone_row == zone_ref[...], 1.0, 0.0).astype(F32)
    stacked = jnp.where(
        row == 0, area * openness_ref[...], jnp.where(row == 1, area, jnp.where(row == 2, area * area, 0.0))
    )
    stat_low[0] = lax.dot_general(
        stacked, member[...], (((1,), (1,)), ((), ())), precision=HIGH, preferred_element_type=F32
    )

    lane = lax.broadcasted_iota(jnp.int32, (ROWS, LANES), 1).astype(F32)

    def build(d):
        columns[d * block : (d + 1) * block, :] = bins[d].T

        def rows_of(r, carry):
            at = pl.multiple_of(d * block + r * ROWS, ROWS)
            mine = columns[pl.ds(at, ROWS), :]
            place = [jnp.broadcast_to(mine[:, k : k + 1], (ROWS, LANES)) - lane for k in range(4)]
            value = [jnp.broadcast_to(mine[:, 4 + k : 5 + k], (ROWS, LANES)) for k in range(4)]
            for c in range(weights.shape[1] // LANES):
                first = float(c * LANES)
                w = jnp.zeros((ROWS, LANES), F32)
                for k in range(4):
                    w = jnp.where(place[k] == first, value[k], w)
                weights[pl.ds(at, ROWS), c * LANES : (c + 1) * LANES] = w.astype(BF16)
            return carry

        lax.fori_loop(0, block // ROWS, rows_of, 0)

    build(0)

    ends = 2 * (1 - lax.rem((h + 1) // 2, 2))
    pl.semaphore_wait(barrier, hours - 1 + SIDE - 1 + YS - 1 + ends)

    def remote(source, held, send, recv, device):
        return pltpu.make_async_remote_copy(
            src_ref=source, dst_ref=held, send_sem=send, recv_sem=recv, device_id=device, device_id_type=MESH
        )

    def spread(buffer, send, recv, device_of):
        copies = [
            remote(buffer.at[0], buffer.at[d], send.at[d], recv.at[d], device_of(d)) for d in range(1, buffer.shape[0])
        ]
        for copy in copies:
            copy.start()
        return copies

    def arrive(copies):
        for copy in copies:
            copy.wait_recv()

    def total_of(buffer, me):
        count = buffer.shape[0]
        total = buffer[me]
        for m in range(1, count):
            total = total + buffer[lax.rem(me + count - m, count)]
        return total

    bins_copies = spread(bins, hour_send.at[0], hour_recv.at[0], hour_of)
    stat_low_copies = spread(stat_low, low_send.at[0], low_recv.at[0], low_of)
    piece = pl.ds(pl.multiple_of(low * PIECE, PIECE), PIECE)
    sky_copies = []
    for d in range(1, hours):
        copy = remote(sky.at[0, piece], sky.at[d, piece], hour_send.at[1, d], hour_recv.at[1, d], hour_of(d))
        copy.start()
        sky_copies.append(copy)
    target_copies = []
    for d in range(1, hours):
        place = pl.ds(pl.multiple_of(lax.rem(h + d, hours) * own, own), own)
        copy = remote(target_hbm.at[:, place], target.at[d], hour_send.at[2, d], hour_recv.at[2, d], hour_of(d))
        copy.start()
        target_copies.append(copy)

    arrive(stat_low_copies)
    stat_y[0] = total_of(stat_low, low)
    stat_y_copies = spread(stat_y, y_send, y_recv, y_of)

    arrive(sky_copies)
    sky_low_copies = []
    for d in range(1, SIDE):
        held = sky.at[1:, piece]
        copy = remote(held, held, low_send.at[1, d], low_recv.at[1, d], low_of(d))
        copy.start()
        sky_low_copies.append(copy)

    arrive(bins_copies)
    for d in range(1, hours):
        build(d)
    for copy in local:
        copy.wait()
    tail_wide[...] = jnp.zeros_like(tail_wide)
    tail_wide[0 : nbins - whole, :] = coef[whole:nbins, :].astype(F32)
    tail[...] = tail_wide[...].astype(BF16)

    arrive(stat_y_copies)
    stat_half[0] = total_of(stat_y, y)
    half_copies = [
        remote(stat_half.at[0], stat_half.at[1], half_send.at[t], half_recv.at[0], taker(t)) for t in range(2)
    ]

    @pl.when(at_end)
    def _():
        for copy in half_copies:
            copy.start()

    for d in range(hours):
        here = slice(d * block, (d + 1) * block)
        cross[d] = jnp.dot(weights[here, 0:whole], coef[0:whole, :], preferred_element_type=F32) + jnp.dot(
            weights[here, whole:], tail[...], preferred_element_type=F32
        )

    arrive(sky_low_copies)
    first = (((0,), (0,)), ((), ()))
    for d in range(hours):
        op_part = lax.dot_general(sky[d, 0:patches], open_own[...], first, preferred_element_type=F32)
        cl_part = lax.dot_general(sky[d, 0:patches], closed_own[...], first, preferred_element_type=F32)
        cross[d] = op_part - cl_part + cross[d]
        lit[d] = cl_part

    half_copies[0].wait_recv()
    sums = stat_half[0] + stat_half[1]
    zone_lane = lax.broadcasted_iota(jnp.int32, (1, LANES), 1)
    den = jnp.where(zone_lane < 2 * PLANE, sums[1:2], 1.0)
    shares = sums[0:1] / den
    share = jnp.sum(jnp.where(zone_lane == s, shares, 0.0), axis=1, keepdims=True)

    lit_copies = []
    for d in (1, 2, 3, 0):
        level = lit[d] + share * cross[d]
        lit[d] = level
        lit_out[d] = level.astype(BF16)
        if d:
            held = lit_hbm.at[:, own_columns]
            copy = remote(lit_out.at[d], held, hour_send.at[3, d], hour_recv.at[3, d], hour_of(hours - d))
            copy.start()
            lit_copies.append(copy)
    own_out = pltpu.make_async_copy(lit_out.at[0], lit_hbm.at[:, own_columns], local_sem.at[0])
    own_out.start()

    terms = jnp.zeros((1, own), F32)
    for d in range(hours):
        if d:
            target_copies[d - 1].wait_recv()
        part = 2.0 * (lit[d] - target[d].astype(F32)) * cross[d]
        terms = terms + jnp.sum(part, axis=0, keepdims=True)
    local_grad = jnp.sum(terms, axis=1, keepdims=True)
    grad_z[0] = jnp.where(zone_lane == s, local_grad, 0.0)
    z_copies = spread(grad_z, z_send, z_recv, z_of)
    arrive(z_copies)
    grad_plane[0] = total_of(grad_z, z)
    plane_copies = spread(grad_plane, plane_send, plane_recv, plane_of)
    arrive(plane_copies)
    zone_grad = total_of(grad_plane, plane)
    ratio = zone_grad / den
    square = jnp.sum(ratio * ratio * sums[2:3], axis=1, keepdims=True)
    rms = jnp.sqrt(square / windows_all + 1e-06)
    spread_ratio = jnp.dot(
        jnp.broadcast_to(ratio, (SIDE, LANES)), member[...], precision=HIGH, preferred_element_type=F32
    )
    grad = area_ref[...] * spread_ratio[0:1]
    new_ref[...] = jnp.clip(openness_ref[...] - 0.25 * grad / rms, 0.0, 1.0)

    for copy in bins_copies + stat_low_copies + sky_copies + target_copies + stat_y_copies + sky_low_copies:
        copy.wait_send()
    for copy in z_copies + plane_copies:
        copy.wait_send()

    @pl.when(at_end)
    def _():
        for copy in half_copies:
            copy.wait_send()

    own_out.wait()
    for copy in lit_copies:
        copy.wait()


def solution(mesh):
    hours = mesh.shape["hour"]
    sens = mesh.shape["sens"]

    def step(sky, sky_open, sky_closed, sun_coef, sun_bins, sun_rad, target, zone_of, area, openness):
        block, patches = sky.shape
        nbins, own = sun_coef.shape
        windows = area.shape[0]
        padded = pl.cdiv(nbins, LANES) * LANES
        any_space = pl.BlockSpec(memory_space=pl.ANY)
        hbm = pl.BlockSpec(memory_space=pltpu.HBM)
        vmem = pl.BlockSpec(memory_space=pltpu.VMEM)
        tile = (SIDE, LANES)
        lit, new = pl.pallas_call(
            functools.partial(kernel, hours, windows * sens),
            out_shape=(
                jax.ShapeDtypeStruct((block, own * hours), BF16),
                jax.ShapeDtypeStruct((1, windows), F32),
            ),
            in_specs=[hbm] * 10,
            out_specs=(any_space, vmem),
            scratch_shapes=[
                pltpu.VMEM(sun_bins.T.shape, jnp.int32),
                pltpu.VMEM(sun_rad.T.shape, BF16),
                pltpu.VMEM((1, windows), jnp.int32),
                pltpu.VMEM((1, windows), F32),
                pltpu.VMEM((1, windows), F32),
                pltpu.VMEM((nbins, own), BF16),
                pltpu.VMEM((LANES, own), F32),
                pltpu.VMEM((LANES, own), BF16),
                pltpu.VMEM((hours * block, padded), BF16),
                pltpu.VMEM((hours * block, SIDE), F32),
                pltpu.VMEM((hours,) + tile, F32),
                pltpu.VMEM((patches, block), BF16),
                pltpu.VMEM((hours, SIDE * PIECE, block), BF16),
                pltpu.VMEM((hours, block, own), BF16),
                pltpu.VMEM((patches, own), BF16),
                pltpu.VMEM((patches, own), BF16),
                pltpu.VMEM((hours, block, own), F32),
                pltpu.VMEM((hours, block, own), F32),
                pltpu.VMEM((hours, block, own), BF16),
                pltpu.VMEM((LANES, windows), F32),
                pltpu.VMEM((SIDE,) + tile, F32),
                pltpu.VMEM((YS,) + tile, F32),
                pltpu.VMEM((2,) + tile, F32),
                pltpu.VMEM((2 * hours, 1, LANES), F32),
                pltpu.VMEM((PLANE, 1, LANES), F32),
                pltpu.SemaphoreType.DMA((16,)),
                pltpu.SemaphoreType.DMA((4, hours)),
                pltpu.SemaphoreType.DMA((4, hours)),
                pltpu.SemaphoreType.DMA((2, SIDE)),
                pltpu.SemaphoreType.DMA((2, SIDE)),
                pltpu.SemaphoreType.DMA((YS,)),
                pltpu.SemaphoreType.DMA((YS,)),
                pltpu.SemaphoreType.DMA((2,)),
                pltpu.SemaphoreType.DMA((1,)),
                pltpu.SemaphoreType.DMA((2 * hours,)),
                pltpu.SemaphoreType.DMA((2 * hours,)),
                pltpu.SemaphoreType.DMA((PLANE,)),
                pltpu.SemaphoreType.DMA((PLANE,)),
            ],
            compiler_params=pltpu.CompilerParams(
                collective_id=0, has_side_effects=True, vmem_limit_bytes=48 << 20
            ),
        )(
            *(
                pltpu.with_memory_space_constraint(x, pltpu.HBM)
                for x in (
                    sky.T,
                    sky_open,
                    sky_closed,
                    sun_coef,
                    sun_bins.T,
                    sun_rad.T,
                    target,
                    zone_of.T,
                    area[None, :],
                    openness[None, :],
                )
            )
        )
        return lit, new[0]

    in_specs = (
        P("hour", None),
        P(None, "sens"),
        P(None, "sens"),
        P(None, ("sens", "hour")),
        P("hour", None),
        P("hour", None),
        P("hour", "sens"),
        P("sens", None),
        P("sens"),
        P("sens"),
    )
    out_specs = (P("hour", "sens"), P("sens"))
    return jax.shard_map(step, mesh=mesh, in_specs=in_specs, out_specs=out_specs, check_vma=False)
```

```python
import functools

import jax
import jax.numpy as jnp
from jax import lax
from jax.experimental import pallas as pl
from jax.experimental.pallas import tpu as pltpu
from jax.sharding import PartitionSpec as P

MESH = pl.DeviceIdType.MESH
F32 = jnp.float32
BF16 = jnp.bfloat16
HIGH = lax.Precision.HIGHEST
SIDE = 8
YS = 4
CORES = 2
PLANE = SIDE * YS
PIECE = 24
LANES = 128
ROWS = 32


def kernel(
    hours,
    windows_all,
    sky_hbm,
    open_hbm,
    closed_hbm,
    coef_hbm,
    bins_hbm,
    rad_hbm,
    target_hbm,
    zone_hbm,
    area_hbm,
    openness_hbm,
    lit_hbm,
    new_ref,
    bins_ref,
    rad_ref,
    zone_ref,
    area_ref,
    openness_ref,
    coef,
    tail_wide,
    tail,
    weights,
    columns,
    bins,
    sky_in,
    sky,
    target,
    open_own,
    closed_own,
    cross,
    lit,
    lit_out,
    member,
    member_half,
    stat_low,
    stat_all,
    grad_column,
    grad_all,
    local_sem,
    hour_send,
    hour_recv,
    low_send,
    low_recv,
    y_send,
    y_recv,
    half_send,
    half_recv,
    column_send,
    column_recv,
    across_send,
    across_recv,
    y_ready,
):
    s = lax.axis_index("sens")
    h = lax.axis_index("hour")
    low = lax.rem(s, SIDE)
    y = lax.rem(s // SIDE, YS)
    plane = lax.rem(s, PLANE)
    half = s // PLANE
    z = half * hours + h
    zs = 2 * hours
    nbins, own = coef.shape
    block = sky.shape[2]
    patches = sky_in.shape[0]
    whole = nbins // LANES * LANES

    def hour_of(d):
        return (s, lax.rem(h + d, hours))

    def low_of(d):
        return (s - low + lax.rem(low + d, SIDE), h)

    def y_of(d):
        return (half * PLANE + lax.rem(y + d, YS) * SIDE + low, h)

    core = lax.rem(s, CORES)
    in_column = z * CORES + core
    chip = plane // CORES

    def column_of(d):
        there = lax.rem(in_column + d, zs * CORES)
        there_z = there // CORES
        return (there_z // hours * PLANE + chip * CORES + lax.rem(there, CORES), lax.rem(there_z, hours))

    def across_of(d):
        return (half * PLANE + lax.rem(chip + d, PLANE // CORES) * CORES + core, h)

    giver = ((1 - half) * PLANE + plane, (hours - 1) * (1 - h // 2))
    at_end = lax.rem(h, hours - 1) == 0
    first_taker = (hours - 1 - h) // (hours - 1) * 2

    def taker(t, there_y):
        return ((1 - half) * PLANE + there_y * SIDE + low, first_taker + t)

    barrier = pltpu.get_barrier_semaphore()
    for d in range(1, hours):
        pl.semaphore_signal(barrier, inc=1, device_id=hour_of(d), device_id_type=MESH)
    pl.semaphore_signal(barrier, inc=1, device_id=giver, device_id_type=MESH)
    for d in range(1, SIDE):
        pl.semaphore_signal(barrier, inc=1, device_id=low_of(d), device_id_type=MESH)
    for d in range(1, YS):
        pl.semaphore_signal(barrier, inc=1, device_id=y_of(d), device_id_type=MESH)

    own_columns = pl.ds(pl.multiple_of(h * own, own), own)
    small = []
    for source, held in (
        (bins_hbm, bins_ref),
        (rad_hbm, rad_ref),
        (sky_hbm, sky_in),
        (zone_hbm, zone_ref),
        (area_hbm, area_ref),
        (openness_hbm, openness_ref),
    ):
        small.append(pltpu.make_async_copy(source, held, local_sem.at[len(small)]))
    local = []
    chunk = 1024
    for at in range(0, nbins, chunk):
        rows = pl.ds(at, min(chunk, nbins - at))
        local.append((coef_hbm.at[rows], coef.at[rows]))
    local.append((open_hbm.at[:, own_columns], open_own))
    local.append((closed_hbm.at[:, own_columns], closed_own))
    local.append((target_hbm.at[:, own_columns], target.at[0]))
    local = [
        pltpu.make_async_copy(source, held, local_sem.at[len(small) + i]) for i, (source, held) in enumerate(local)
    ]
    for copy in small + local:
        copy.start()
    for copy in small:
        copy.wait()

    bins[0, 0:4, :] = bins_ref[...].astype(F32)
    bins[0, 4:8, :] = rad_ref[...].astype(F32)
    sky[0, patches // 16 * 16 :, :] = jnp.zeros_like(sky[0, patches // 16 * 16 :, :])
    sky[0, 0:patches, :] = sky_in[...]

    area = area_ref[...]
    row = lax.broadcasted_iota(jnp.int32, (SIDE, area.shape[1]), 0)
    zone_row = lax.broadcasted_iota(jnp.int32, member.shape, 0)
    member[...] = jnp.where(zone_row == zone_ref[...], 1.0, 0.0).astype(F32)
    member_half[...] = member[...].astype(BF16)
    stacked = jnp.where(
        row == 0, area * openness_ref[...], jnp.where(row == 1, area, jnp.where(row == 2, area * area, 0.0))
    )
    stat_low[low] = lax.dot_general(
        stacked, member[...], (((1,), (1,)), ((), ())), precision=HIGH, preferred_element_type=F32
    )

    lane = lax.broadcasted_iota(jnp.int32, (ROWS, LANES), 1).astype(F32)

    def build(d):
        columns[d * block : (d + 1) * block, :] = bins[d].T

        def rows_of(r, carry):
            at = pl.multiple_of(d * block + r * ROWS, ROWS)
            mine = columns[pl.ds(at, ROWS), :]
            place = [jnp.broadcast_to(mine[:, k : k + 1], (ROWS, LANES)) - lane for k in range(4)]
            value = [jnp.broadcast_to(mine[:, 4 + k : 5 + k], (ROWS, LANES)) for k in range(4)]
            for c in range(weights.shape[1] // LANES):
                first = float(c * LANES)
                w = jnp.zeros((ROWS, LANES), F32)
                for k in range(4):
                    w = jnp.where(place[k] == first, value[k], w)
                weights[pl.ds(at, ROWS), c * LANES : (c + 1) * LANES] = w.astype(BF16)
            return carry

        lax.fori_loop(0, block // ROWS, rows_of, 0)

    build(0)

    ends = 2 * (1 - lax.rem((h + 1) // 2, 2))
    pl.semaphore_wait(barrier, hours - 1 + SIDE - 1 + YS - 1 + ends)

    def remote(source, held, send, recv, device):
        return pltpu.make_async_remote_copy(
            src_ref=source, dst_ref=held, send_sem=send, recv_sem=recv, device_id=device, device_id_type=MESH
        )

    def spread(buffer, me, send, recv, device_of):
        mine = buffer.at[me]
        copies = [remote(mine, mine, send.at[d], recv.at[d], device_of(d)) for d in range(1, buffer.shape[0])]
        for copy in copies:
            copy.start()
        return copies

    def arrive(copies):
        for copy in copies:
            copy.wait_recv()

    def total_of(buffer):
        total = buffer[0]
        for m in range(1, buffer.shape[0]):
            total = total + buffer[m]
        return total

    stat_low_copies = spread(stat_low, low, low_send.at[0], low_recv.at[0], low_of)
    for d in range(1, YS):
        pl.semaphore_signal(y_ready, inc=1, device_id=y_of(d), device_id_type=MESH)
    bins_copies = []
    for d in range(1, hours):
        copy = remote(bins.at[0], bins.at[d], hour_send.at[0, d], hour_recv.at[0, d], hour_of(d))
        copy.start()
        bins_copies.append(copy)
    piece = pl.ds(pl.multiple_of(low * PIECE, PIECE), PIECE)
    sky_copies = []
    for d in range(1, hours):
        copy = remote(sky.at[0, piece], sky.at[d, piece], hour_send.at[1, d], hour_recv.at[1, d], hour_of(d))
        copy.start()
        sky_copies.append(copy)
    target_copies = []
    for d in range(1, hours):
        place = pl.ds(pl.multiple_of(lax.rem(h + d, hours) * own, own), own)
        copy = remote(target_hbm.at[:, place], target.at[d], hour_send.at[2, d], hour_recv.at[2, d], hour_of(d))
        copy.start()
        target_copies.append(copy)

    arrive(stat_low_copies)
    group = half * YS + y
    stat_all[group] = total_of(stat_low)
    mine = stat_all.at[group]
    stat_y_copies = []
    for d in range(1, YS):
        copy = remote(mine, mine, y_send.at[d], y_recv.at[d], y_of(d))
        copy.start()
        stat_y_copies.append(copy)
    pl.semaphore_wait(y_ready, YS - 1)
    half_copies = [
        remote(mine, mine, half_send.at[t, there_y], half_recv.at[y], taker(t, there_y))
        for there_y in range(YS)
        for t in range(2)
    ]

    @pl.when(at_end)
    def _():
        for copy in half_copies:
            copy.start()

    arrive(sky_copies)
    sky_low_copies = []
    for d in range(1, SIDE):
        held = sky.at[1:, piece]
        copy = remote(held, held, low_send.at[1, d], low_recv.at[1, d], low_of(d))
        copy.start()
        sky_low_copies.append(copy)

    arrive(bins_copies)
    for d in range(1, hours):
        build(d)
    for copy in local:
        copy.wait()
    tail_wide[...] = jnp.zeros_like(tail_wide)
    tail_wide[0 : nbins - whole, :] = coef[whole:nbins, :].astype(F32)
    tail[...] = tail_wide[...].astype(BF16)

    for d in range(hours):
        here = slice(d * block, (d + 1) * block)
        cross[d] = jnp.dot(weights[here, 0:whole], coef[0:whole, :], preferred_element_type=F32) + jnp.dot(
            weights[here, whole:], tail[...], preferred_element_type=F32
        )

    arrive(sky_low_copies)
    first = (((0,), (0,)), ((), ()))
    for d in range(hours):
        op_part = lax.dot_general(sky[d, 0:patches], open_own[...], first, preferred_element_type=F32)
        cl_part = lax.dot_general(sky[d, 0:patches], closed_own[...], first, preferred_element_type=F32)
        cross[d] = op_part - cl_part + cross[d]
        lit[d] = cl_part

    arrive(stat_y_copies)
    for there_y in range(YS):
        remote(mine, mine, half_send.at[0, 0], half_recv.at[there_y], taker(0, 0)).wait_recv()
    sums = total_of(stat_all)
    zone_lane = lax.broadcasted_iota(jnp.int32, (1, LANES), 1)
    den = jnp.where(zone_lane < 2 * PLANE, sums[1:2], 1.0)
    shares = sums[0:1] / den
    share = jnp.sum(jnp.where(zone_lane == s, shares, 0.0), axis=1, keepdims=True)

    for d in range(hours):
        level = lit[d] + share * cross[d]
        lit[d] = level
        lit_out[d] = level.astype(BF16)
    own_out = pltpu.make_async_copy(lit_out.at[0], lit_hbm.at[:, own_columns], local_sem.at[0])
    own_out.start()

    terms = jnp.zeros((1, own), F32)
    for d in range(hours):
        if d:
            target_copies[d - 1].wait_recv()
        part = 2.0 * (lit[d] - target[d].astype(F32)) * cross[d]
        terms = terms + jnp.sum(part, axis=0, keepdims=True)
    local_grad = jnp.sum(terms, axis=1, keepdims=True)
    grad_column[in_column] = jnp.where(zone_lane == s, local_grad, 0.0)
    column_copies = spread(grad_column, in_column, column_send, column_recv, column_of)
    lit_copies = []
    for d in range(1, hours):
        held = lit_hbm.at[:, own_columns]
        copy = remote(lit_out.at[d], held, hour_send.at[3, d], hour_recv.at[3, d], hour_of(hours - d))
        copy.start()
        lit_copies.append(copy)
    arrive(column_copies)
    grad_all[chip] = total_of(grad_column)
    across_copies = spread(grad_all, chip, across_send, across_recv, across_of)
    arrive(across_copies)
    zone_grad = total_of(grad_all)
    ratio = zone_grad / den
    square = jnp.sum(ratio * ratio * sums[2:3], axis=1, keepdims=True)
    rms = jnp.sqrt(square / windows_all + 1e-06)
    first_part = ratio.astype(BF16).astype(F32)
    second_part = (ratio - first_part).astype(BF16).astype(F32)
    third_part = ratio - first_part - second_part
    part_row = lax.broadcasted_iota(jnp.int32, (16, LANES), 0)
    parts = jnp.where(part_row == 0, first_part, jnp.where(part_row == 1, second_part, third_part))
    parts = jnp.where(part_row < 3, parts, 0.0).astype(BF16)
    chosen = jnp.dot(parts, member_half[...], preferred_element_type=F32)
    chosen = chosen[0:1] + chosen[1:2] + chosen[2:3]
    grad = area_ref[...] * chosen
    new_ref[...] = jnp.clip(openness_ref[...] - 0.25 * grad / rms, 0.0, 1.0)

    for copy in bins_copies + stat_low_copies + sky_copies + target_copies + stat_y_copies + sky_low_copies:
        copy.wait_send()
    for copy in column_copies + across_copies:
        copy.wait_send()

    @pl.when(at_end)
    def _():
        for copy in half_copies:
            copy.wait_send()

    own_out.wait()
    for copy in lit_copies:
        copy.wait()


def solution(mesh):
    hours = mesh.shape["hour"]
    sens = mesh.shape["sens"]

    def step(sky, sky_open, sky_closed, sun_coef, sun_bins, sun_rad, target, zone_of, area, openness):
        block, patches = sky.shape
        nbins, own = sun_coef.shape
        windows = area.shape[0]
        padded = pl.cdiv(nbins, LANES) * LANES
        any_space = pl.BlockSpec(memory_space=pl.ANY)
        hbm = pl.BlockSpec(memory_space=pltpu.HBM)
        vmem = pl.BlockSpec(memory_space=pltpu.VMEM)
        tile = (SIDE, LANES)
        lit, new = pl.pallas_call(
            functools.partial(kernel, hours, windows * sens),
            out_shape=(
                jax.ShapeDtypeStruct((block, own * hours), BF16),
                jax.ShapeDtypeStruct((1, windows), F32),
            ),
            in_specs=[hbm] * 10,
            out_specs=(any_space, vmem),
            scratch_shapes=[
                pltpu.VMEM(sun_bins.T.shape, jnp.int32),
                pltpu.VMEM(sun_rad.T.shape, BF16),
                pltpu.VMEM((1, windows), jnp.int32),
                pltpu.VMEM((1, windows), F32),
                pltpu.VMEM((1, windows), F32),
                pltpu.VMEM((nbins, own), BF16),
                pltpu.VMEM((LANES, own), F32),
                pltpu.VMEM((LANES, own), BF16),
                pltpu.VMEM((hours * block, padded), BF16),
                pltpu.VMEM((hours * block, SIDE), F32),
                pltpu.VMEM((hours,) + tile, F32),
                pltpu.VMEM((patches, block), BF16),
                pltpu.VMEM((hours, SIDE * PIECE, block), BF16),
                pltpu.VMEM((hours, block, own), BF16),
                pltpu.VMEM((patches, own), BF16),
                pltpu.VMEM((patches, own), BF16),
                pltpu.VMEM((hours, block, own), F32),
                pltpu.VMEM((hours, block, own), F32),
                pltpu.VMEM((hours, block, own), BF16),
                pltpu.VMEM((LANES, windows), F32),
                pltpu.VMEM((LANES, windows), BF16),
                pltpu.VMEM((SIDE,) + tile, F32),
                pltpu.VMEM((2 * YS,) + tile, F32),
                pltpu.VMEM((2 * hours * CORES, 1, LANES), F32),
                pltpu.VMEM((PLANE // CORES, 1, LANES), F32),
                pltpu.SemaphoreType.DMA((16,)),
                pltpu.SemaphoreType.DMA((4, hours)),
                pltpu.SemaphoreType.DMA((4, hours)),
                pltpu.SemaphoreType.DMA((2, SIDE)),
                pltpu.SemaphoreType.DMA((2, SIDE)),
                pltpu.SemaphoreType.DMA((YS,)),
                pltpu.SemaphoreType.DMA((YS,)),
                pltpu.SemaphoreType.DMA((2, YS)),
                pltpu.SemaphoreType.DMA((YS,)),
                pltpu.SemaphoreType.DMA((2 * hours * CORES,)),
                pltpu.SemaphoreType.DMA((2 * hours * CORES,)),
                pltpu.SemaphoreType.DMA((PLANE // CORES,)),
                pltpu.SemaphoreType.DMA((PLANE // CORES,)),
                pltpu.SemaphoreType.REGULAR,
            ],
            compiler_params=pltpu.CompilerParams(
                collective_id=0, has_side_effects=True, vmem_limit_bytes=48 << 20
            ),
        )(
            *(
                pltpu.with_memory_space_constraint(x, pltpu.HBM)
                for x in (
                    sky.T,
                    sky_open,
                    sky_closed,
                    sun_coef,
                    sun_bins.T,
                    sun_rad.T,
                    target,
                    zone_of.T,
                    area[None, :],
                    openness[None, :],
                )
            )
        )
        return lit, new[0]

    in_specs = (
        P("hour", None),
        P(None, "sens"),
        P(None, "sens"),
        P(None, ("sens", "hour")),
        P("hour", None),
        P("hour", None),
        P("hour", "sens"),
        P("sens", None),
        P("sens"),
        P("sens"),
    )
    out_specs = (P("hour", "sens"), P("sens"))
    return jax.shard_map(step, mesh=mesh, in_specs=in_specs, out_specs=out_specs, check_vma=False)
```

```python
import functools

import jax
import jax.numpy as jnp
from jax import lax
from jax.experimental import pallas as pl
from jax.experimental.pallas import tpu as pltpu
from jax.sharding import PartitionSpec as P

MESH = pl.DeviceIdType.MESH
F32 = jnp.float32
BF16 = jnp.bfloat16
HIGH = lax.Precision.HIGHEST
SIDE = 8
YS = 4
CORES = 2
XS = 4
PLANE = SIDE * YS
PIECE = 24
LANES = 128
ROWS = 32


def kernel(
    hours,
    windows_all,
    sky_hbm,
    open_hbm,
    closed_hbm,
    coef_hbm,
    bins_hbm,
    rad_hbm,
    target_hbm,
    zone_hbm,
    area_hbm,
    openness_hbm,
    lit_hbm,
    new_ref,
    bins_ref,
    rad_ref,
    zone_ref,
    area_ref,
    openness_ref,
    coef,
    tail_wide,
    tail,
    weights,
    columns,
    bins,
    sky_in,
    sky,
    target,
    open_own,
    closed_own,
    cross,
    lit,
    lit_out,
    member,
    stat_low,
    stat_all,
    grad_column,
    grad_all,
    local_sem,
    hour_send,
    hour_recv,
    low_send,
    low_recv,
    y_send,
    y_recv,
    half_send,
    half_recv,
    column_send,
    column_recv,
    across_send,
    across_recv,
    y_ready,
):
    s = lax.axis_index("sens")
    h = lax.axis_index("hour")
    low = lax.rem(s, SIDE)
    y = lax.rem(lax.div(s, SIDE), YS)
    plane = lax.rem(s, PLANE)
    half = lax.div(s, PLANE)
    z = half * hours + h
    zs = 2 * hours
    nbins, own = coef.shape
    block = sky.shape[2]
    patches = sky_in.shape[0]
    whole = nbins // LANES * LANES

    def hour_of(d):
        return (s, lax.rem(h + d, hours))

    def low_of(d):
        return (s - low + lax.rem(low + d, SIDE), h)

    def y_of(d):
        return (half * PLANE + lax.rem(y + d, YS) * SIDE + low, h)

    core = lax.rem(s, CORES)
    in_column = z * CORES + core
    chip = lax.div(plane, CORES)
    chip_x = lax.rem(chip, XS)
    columns_z = [lax.rem(z + d, zs) for d in range(zs)]
    columns_z = [(lax.div(there, hours) * PLANE + chip * CORES, lax.rem(there, hours)) for there in columns_z]
    columns_core = [core, 1 - core]
    across_y = [half * PLANE + lax.rem(y + d, YS) * SIDE + core for d in range(YS)]
    across_x = [lax.rem(chip_x + d, XS) * CORES for d in range(XS)]

    def column_of(d):
        first, there = columns_z[d // CORES]
        return (first + columns_core[d % CORES], there)

    def across_of(d):
        return (across_y[d // XS] + across_x[d % XS], h)

    giver = ((1 - half) * PLANE + plane, (hours - 1) * (1 - lax.div(h, 2)))
    at_end = lax.rem(h, hours - 1) == 0
    first_taker = lax.div(hours - 1 - h, hours - 1) * 2

    def taker(t, there_y):
        return ((1 - half) * PLANE + there_y * SIDE + low, first_taker + t)

    barrier = pltpu.get_barrier_semaphore()
    for d in range(1, hours):
        pl.semaphore_signal(barrier, inc=1, device_id=hour_of(d), device_id_type=MESH)
    pl.semaphore_signal(barrier, inc=1, device_id=giver, device_id_type=MESH)
    for d in range(1, SIDE):
        pl.semaphore_signal(barrier, inc=1, device_id=low_of(d), device_id_type=MESH)
    for d in range(1, YS):
        pl.semaphore_signal(barrier, inc=1, device_id=y_of(d), device_id_type=MESH)

    own_columns = pl.ds(pl.multiple_of(h * own, own), own)
    small = []
    for source, held in (
        (bins_hbm, bins_ref),
        (rad_hbm, rad_ref),
        (sky_hbm, sky_in),
        (zone_hbm, zone_ref),
        (area_hbm, area_ref),
        (openness_hbm, openness_ref),
    ):
        small.append(pltpu.make_async_copy(source, held, local_sem.at[len(small)]))
    local = []
    chunk = 1024
    for at in range(0, nbins, chunk):
        rows = pl.ds(at, min(chunk, nbins - at))
        local.append((coef_hbm.at[rows], coef.at[rows]))
    local.append((open_hbm.at[:, own_columns], open_own))
    local.append((closed_hbm.at[:, own_columns], closed_own))
    local.append((target_hbm.at[:, own_columns], target.at[0]))
    local = [
        pltpu.make_async_copy(source, held, local_sem.at[len(small) + i]) for i, (source, held) in enumerate(local)
    ]
    for copy in small + local:
        copy.start()
    for copy in small[:3]:
        copy.wait()

    bins[0, 0:4, :] = bins_ref[...].astype(F32)
    bins[0, 4:8, :] = rad_ref[...].astype(F32)
    sky[0, patches // 16 * 16 :, :] = jnp.zeros_like(sky[0, patches // 16 * 16 :, :])
    sky[0, 0:patches, :] = sky_in[...]

    lane = lax.broadcasted_iota(jnp.int32, (ROWS, LANES), 1).astype(F32)

    def build(d):
        columns[d * block : (d + 1) * block, :] = bins[d].T

        def rows_of(r, carry):
            at = pl.multiple_of(d * block + r * ROWS, ROWS)
            mine = columns[pl.ds(at, ROWS), :]
            place = [jnp.broadcast_to(mine[:, k : k + 1], (ROWS, LANES)) - lane for k in range(4)]
            value = [jnp.broadcast_to(mine[:, 4 + k : 5 + k], (ROWS, LANES)) for k in range(4)]
            for c in range(weights.shape[1] // LANES):
                first = float(c * LANES)
                w = jnp.zeros((ROWS, LANES), F32)
                for k in range(4):
                    w = jnp.where(place[k] == first, value[k], w)
                weights[pl.ds(at, ROWS), c * LANES : (c + 1) * LANES] = w.astype(BF16)
            return carry

        lax.fori_loop(0, block // ROWS, rows_of, 0)

    ends = 2 * (1 - lax.rem(lax.div(h + 1, 2), 2))
    pl.semaphore_wait(barrier, hours - 1 + SIDE - 1 + YS - 1 + ends)

    def remote(source, held, send, recv, device):
        return pltpu.make_async_remote_copy(
            src_ref=source, dst_ref=held, send_sem=send, recv_sem=recv, device_id=device, device_id_type=MESH
        )

    def spread(buffer, me, send, recv, device_of):
        mine = buffer.at[me]
        copies = [remote(mine, mine, send.at[d], recv.at[d], device_of(d)) for d in range(1, buffer.shape[0])]
        for copy in copies:
            copy.start()
        return copies

    def arrive(copies):
        for copy in copies:
            copy.wait_recv()

    def total_of(buffer):
        total = buffer[0]
        for m in range(1, buffer.shape[0]):
            total = total + buffer[m]
        return total

    bins_copies = []
    for d in range(1, hours):
        copy = remote(bins.at[0], bins.at[d], hour_send.at[0, d], hour_recv.at[0, d], hour_of(d))
        copy.start()
        bins_copies.append(copy)
    piece = pl.ds(pl.multiple_of(low * PIECE, PIECE), PIECE)
    sky_copies = []
    for d in range(1, hours):
        copy = remote(sky.at[0, piece], sky.at[d, piece], hour_send.at[1, d], hour_recv.at[1, d], hour_of(d))
        copy.start()
        sky_copies.append(copy)
    target_copies = []
    for d in range(1, hours):
        place = pl.ds(pl.multiple_of(lax.rem(h + d, hours) * own, own), own)
        copy = remote(target_hbm.at[:, place], target.at[d], hour_send.at[2, d], hour_recv.at[2, d], hour_of(d))
        copy.start()
        target_copies.append(copy)

    for copy in small[3:]:
        copy.wait()
    area = area_ref[...]
    zone_row = lax.broadcasted_iota(jnp.int32, member.shape, 0)
    member[...] = jnp.where(zone_row == zone_ref[...], 1.0, 0.0).astype(BF16)

    def parts_of(value):
        first = value.astype(BF16).astype(F32)
        second = (value - first).astype(BF16).astype(F32)
        return first, second, value - first - second

    row = lax.broadcasted_iota(jnp.int32, (16, area.shape[1]), 0)
    stacked = jnp.zeros(row.shape, F32)
    for i, value in enumerate((area * openness_ref[...], area, area * area)):
        for part, rest in enumerate(parts_of(value)):
            stacked = jnp.where(row == 4 * part + i, rest, stacked)
    partial = lax.dot_general(
        stacked.astype(BF16), member[...], (((1,), (1,)), ((), ())), preferred_element_type=F32
    )
    stat_low[low, 0:4] = partial[0:4] + partial[4:8] + partial[8:12]
    stat_low[low, 4:8] = jnp.zeros((4, LANES), F32)

    stat_low_copies = spread(stat_low, low, low_send.at[0], low_recv.at[0], low_of)
    for d in range(1, YS):
        pl.semaphore_signal(y_ready, inc=1, device_id=y_of(d), device_id_type=MESH)
    def sun_of(d):
        here = slice(d * block, (d + 1) * block)
        cross[d] = jnp.dot(weights[here, 0:whole], coef[0:whole, :], preferred_element_type=F32) + jnp.dot(
            weights[here, whole:], tail[...], preferred_element_type=F32
        )

    def levels_of(d):
        first = (((0,), (0,)), ((), ()))
        op_part = lax.dot_general(sky[d, 0:patches], open_own[...], first, preferred_element_type=F32)
        cl_part = lax.dot_general(sky[d, 0:patches], closed_own[...], first, preferred_element_type=F32)
        cross[d] = op_part - cl_part + cross[d]
        lit[d] = cl_part

    build(0)
    for copy in local:
        copy.wait()
    tail_wide[...] = jnp.zeros_like(tail_wide)
    tail_wide[0 : nbins - whole, :] = coef[whole:nbins, :].astype(F32)
    tail[...] = tail_wide[...].astype(BF16)
    sun_of(0)
    levels_of(0)

    arrive(stat_low_copies)
    group = half * YS + y
    stat_all[group] = total_of(stat_low)
    mine = stat_all.at[group]
    stat_y_copies = []
    for d in range(1, YS):
        copy = remote(mine, mine, y_send.at[d], y_recv.at[d], y_of(d))
        copy.start()
        stat_y_copies.append(copy)
    pl.semaphore_wait(y_ready, YS - 1)
    half_copies = [
        remote(mine, mine, half_send.at[t, there_y], half_recv.at[y], taker(t, there_y))
        for there_y in range(YS)
        for t in range(2)
    ]

    @pl.when(at_end)
    def _():
        for copy in half_copies:
            copy.start()

    arrive(sky_copies)
    sky_low_copies = []
    for d in range(1, SIDE):
        held = sky.at[1:, piece]
        copy = remote(held, held, low_send.at[1, d], low_recv.at[1, d], low_of(d))
        copy.start()
        sky_low_copies.append(copy)

    arrive(bins_copies)
    for d in range(1, hours):
        build(d)
    for d in range(1, hours):
        sun_of(d)
    arrive(sky_low_copies)
    for d in range(1, hours):
        levels_of(d)

    arrive(stat_y_copies)
    for there_y in range(YS):
        remote(mine, mine, half_send.at[0, 0], half_recv.at[there_y], taker(0, 0)).wait_recv()
    sums = total_of(stat_all)
    zone_lane = lax.broadcasted_iota(jnp.int32, (1, LANES), 1)
    den = jnp.where(zone_lane < 2 * PLANE, sums[1:2], 1.0)
    shares = sums[0:1] / den
    share = jnp.sum(jnp.where(zone_lane == s, shares, 0.0), axis=1, keepdims=True)

    for d in range(hours):
        level = lit[d] + share * cross[d]
        lit[d] = level
        lit_out[d] = level.astype(BF16)
    own_out = pltpu.make_async_copy(lit_out.at[0], lit_hbm.at[:, own_columns], local_sem.at[0])
    own_out.start()

    terms = jnp.zeros((1, own), F32)
    for d in range(hours):
        if d:
            target_copies[d - 1].wait_recv()
        part = 2.0 * (lit[d] - target[d].astype(F32)) * cross[d]
        terms = terms + jnp.sum(part, axis=0, keepdims=True)
    local_grad = jnp.sum(terms, axis=1, keepdims=True)
    grad_column[in_column] = jnp.where(zone_lane == s, local_grad, 0.0)
    column_copies = spread(grad_column, in_column, column_send, column_recv, column_of)
    lit_copies = []
    for d in range(1, hours):
        held = lit_hbm.at[:, own_columns]
        copy = remote(lit_out.at[d], held, hour_send.at[3, d], hour_recv.at[3, d], hour_of(hours - d))
        copy.start()
        lit_copies.append(copy)
    arrive(column_copies)
    grad_all[chip] = total_of(grad_column)
    across_copies = spread(grad_all, chip, across_send, across_recv, across_of)
    arrive(across_copies)
    zone_grad = total_of(grad_all)
    ratio = zone_grad / den
    square = jnp.sum(ratio * ratio * sums[2:3], axis=1, keepdims=True)
    rms = jnp.sqrt(square / windows_all + 1e-06)
    first_part, second_part, third_part = parts_of(ratio)
    part_row = lax.broadcasted_iota(jnp.int32, (16, LANES), 0)
    parts = jnp.where(part_row == 0, first_part, jnp.where(part_row == 1, second_part, third_part))
    parts = jnp.where(part_row < 3, parts, 0.0).astype(BF16)
    chosen = jnp.dot(parts, member[...], preferred_element_type=F32)
    chosen = chosen[0:1] + chosen[1:2] + chosen[2:3]
    grad = area_ref[...] * chosen
    new_ref[...] = jnp.clip(openness_ref[...] - 0.25 * grad / rms, 0.0, 1.0)

    for copy in bins_copies + stat_low_copies + sky_copies + target_copies + stat_y_copies + sky_low_copies:
        copy.wait_send()
    for copy in column_copies + across_copies:
        copy.wait_send()

    @pl.when(at_end)
    def _():
        for copy in half_copies:
            copy.wait_send()

    own_out.wait()
    for copy in lit_copies:
        copy.wait()


def hand_over(lit_in, new_in, lit_hbm, new_hbm, sem):
    copies = [pltpu.make_async_copy(lit_in, lit_hbm, sem.at[0]), pltpu.make_async_copy(new_in, new_hbm, sem.at[1])]
    for copy in copies:
        copy.start()
    for copy in copies:
        copy.wait()


def solution(mesh):
    hours = mesh.shape["hour"]
    sens = mesh.shape["sens"]

    def step(sky, sky_open, sky_closed, sun_coef, sun_bins, sun_rad, target, zone_of, area, openness):
        block, patches = sky.shape
        nbins, own = sun_coef.shape
        windows = area.shape[0]
        padded = pl.cdiv(nbins, LANES) * LANES
        any_space = pl.BlockSpec(memory_space=pl.ANY)
        hbm = pl.BlockSpec(memory_space=pltpu.HBM)
        vmem = pl.BlockSpec(memory_space=pltpu.VMEM)
        tile = (SIDE, LANES)
        lit, new = pl.pallas_call(
            functools.partial(kernel, hours, windows * sens),
            out_shape=(
                jax.ShapeDtypeStruct((block, own * hours), BF16),
                jax.ShapeDtypeStruct((1, windows), F32),
            ),
            in_specs=[hbm] * 10,
            out_specs=(any_space, vmem),
            scratch_shapes=[
                pltpu.VMEM(sun_bins.T.shape, jnp.int32),
                pltpu.VMEM(sun_rad.T.shape, BF16),
                pltpu.VMEM((1, windows), jnp.int32),
                pltpu.VMEM((1, windows), F32),
                pltpu.VMEM((1, windows), F32),
                pltpu.VMEM((nbins, own), BF16),
                pltpu.VMEM((LANES, own), F32),
                pltpu.VMEM((LANES, own), BF16),
                pltpu.VMEM((hours * block, padded), BF16),
                pltpu.VMEM((hours * block, SIDE), F32),
                pltpu.VMEM((hours,) + tile, F32),
                pltpu.VMEM((patches, block), BF16),
                pltpu.VMEM((hours, SIDE * PIECE, block), BF16),
                pltpu.VMEM((hours, block, own), BF16),
                pltpu.VMEM((patches, own), BF16),
                pltpu.VMEM((patches, own), BF16),
                pltpu.VMEM((hours, block, own), F32),
                pltpu.VMEM((hours, block, own), F32),
                pltpu.VMEM((hours, block, own), BF16),
                pltpu.VMEM((LANES, windows), BF16),
                pltpu.VMEM((SIDE,) + tile, F32),
                pltpu.VMEM((2 * YS,) + tile, F32),
                pltpu.VMEM((2 * hours * CORES, 1, LANES), F32),
                pltpu.VMEM((PLANE // CORES, 1, LANES), F32),
                pltpu.SemaphoreType.DMA((16,)),
                pltpu.SemaphoreType.DMA((4, hours)),
                pltpu.SemaphoreType.DMA((4, hours)),
                pltpu.SemaphoreType.DMA((2, SIDE)),
                pltpu.SemaphoreType.DMA((2, SIDE)),
                pltpu.SemaphoreType.DMA((YS,)),
                pltpu.SemaphoreType.DMA((YS,)),
                pltpu.SemaphoreType.DMA((2, YS)),
                pltpu.SemaphoreType.DMA((YS,)),
                pltpu.SemaphoreType.DMA((2 * hours * CORES,)),
                pltpu.SemaphoreType.DMA((2 * hours * CORES,)),
                pltpu.SemaphoreType.DMA((PLANE // CORES,)),
                pltpu.SemaphoreType.DMA((PLANE // CORES,)),
                pltpu.SemaphoreType.REGULAR,
            ],
            compiler_params=pltpu.CompilerParams(
                collective_id=0, has_side_effects=True, vmem_limit_bytes=48 << 20
            ),
        )(
            *(
                pltpu.with_memory_space_constraint(x, pltpu.HBM)
                for x in (
                    sky.T,
                    sky_open,
                    sky_closed,
                    sun_coef,
                    sun_bins.T,
                    sun_rad.T,
                    target,
                    zone_of.T,
                    area[None, :],
                    openness[None, :],
                )
            )
        )
        lit, new = pl.pallas_call(
            hand_over,
            out_shape=(jax.ShapeDtypeStruct(lit.shape, BF16), jax.ShapeDtypeStruct(new.shape, F32)),
            in_specs=[vmem, vmem],
            out_specs=(any_space, any_space),
            scratch_shapes=[pltpu.SemaphoreType.DMA((2,))],
            compiler_params=pltpu.CompilerParams(vmem_limit_bytes=1 << 20),
        )(lit, new)
        return lit, new[0]

    in_specs = (
        P("hour", None),
        P(None, "sens"),
        P(None, "sens"),
        P(None, ("sens", "hour")),
        P("hour", None),
        P("hour", None),
        P("hour", "sens"),
        P("sens", None),
        P("sens"),
        P("sens"),
    )
    out_specs = (P("hour", "sens"), P("sens"))
    return jax.shard_map(step, mesh=mesh, in_specs=in_specs, out_specs=out_specs, check_vma=False)
```

```python
import functools

import jax
import jax.numpy as jnp
from jax import lax
from jax.experimental import pallas as pl
from jax.experimental.pallas import tpu as pltpu
from jax.sharding import PartitionSpec as P

MESH = pl.DeviceIdType.MESH
F32 = jnp.float32
BF16 = jnp.bfloat16
HIGH = lax.Precision.HIGHEST
SIDE = 8
YS = 4
CORES = 2
XS = 4
PLANE = SIDE * YS
PIECE = 24
LANES = 128
ROWS = 32


def kernel(
    hours,
    windows_all,
    sky_hbm,
    open_hbm,
    closed_hbm,
    coef_hbm,
    bins_hbm,
    rad_hbm,
    target_hbm,
    zone_hbm,
    area_hbm,
    openness_hbm,
    lit_hbm,
    new_ref,
    bins_ref,
    rad_ref,
    zone_ref,
    area_ref,
    openness_ref,
    coef,
    tail_wide,
    tail,
    weights,
    columns,
    bins,
    sky_in,
    sky,
    target,
    open_own,
    closed_own,
    cross,
    lit,
    lit_out,
    member,
    stat_low,
    stat_all,
    grad_column,
    grad_all,
    local_sem,
    hour_send,
    hour_recv,
    low_send,
    low_recv,
    y_send,
    y_recv,
    half_send,
    half_recv,
    column_send,
    column_recv,
    across_send,
    across_recv,
    y_ready,
):
    s = lax.axis_index("sens")
    h = lax.axis_index("hour")
    low = lax.rem(s, SIDE)
    y = lax.rem(lax.div(s, SIDE), YS)
    plane = lax.rem(s, PLANE)
    half = lax.div(s, PLANE)
    z = half * hours + h
    zs = 2 * hours
    nbins, own = coef.shape
    block = sky.shape[2]
    patches = sky_in.shape[0]
    whole = nbins // LANES * LANES

    def hour_of(d):
        return (s, lax.rem(h + d, hours))

    def low_of(d):
        return (s - low + lax.rem(low + d, SIDE), h)

    def y_of(d):
        return (half * PLANE + lax.rem(y + d, YS) * SIDE + low, h)

    core = lax.rem(s, CORES)
    in_column = z * CORES + core
    chip = lax.div(plane, CORES)
    chip_x = lax.rem(chip, XS)
    columns_z = [lax.rem(z + d, zs) for d in range(zs)]
    columns_z = [(lax.div(there, hours) * PLANE + chip * CORES, lax.rem(there, hours)) for there in columns_z]
    columns_core = [core, 1 - core]
    across_y = [half * PLANE + lax.rem(y + d, YS) * SIDE + core for d in range(YS)]
    across_x = [lax.rem(chip_x + d, XS) * CORES for d in range(XS)]

    def column_of(d):
        first, there = columns_z[d // CORES]
        return (first + columns_core[d % CORES], there)

    def across_of(d):
        return (across_y[d // XS] + across_x[d % XS], h)

    giver = ((1 - half) * PLANE + plane, (hours - 1) * (1 - lax.div(h, 2)))
    at_end = lax.rem(h, hours - 1) == 0
    first_taker = lax.div(hours - 1 - h, hours - 1) * 2

    def taker(t, there_y):
        return ((1 - half) * PLANE + there_y * SIDE + low, first_taker + t)

    barrier = pltpu.get_barrier_semaphore()
    for d in range(1, hours):
        pl.semaphore_signal(barrier, inc=1, device_id=hour_of(d), device_id_type=MESH)
    pl.semaphore_signal(barrier, inc=1, device_id=giver, device_id_type=MESH)
    for d in range(1, SIDE):
        pl.semaphore_signal(barrier, inc=1, device_id=low_of(d), device_id_type=MESH)
    for d in range(1, YS):
        pl.semaphore_signal(barrier, inc=1, device_id=y_of(d), device_id_type=MESH)

    own_columns = pl.ds(pl.multiple_of(h * own, own), own)
    small = []
    for source, held in (
        (bins_hbm, bins_ref),
        (rad_hbm, rad_ref),
        (sky_hbm, sky_in),
        (zone_hbm, zone_ref),
        (area_hbm, area_ref),
        (openness_hbm, openness_ref),
    ):
        small.append(pltpu.make_async_copy(source, held, local_sem.at[len(small)]))
    local = []
    chunk = 1024
    for at in range(0, nbins, chunk):
        rows = pl.ds(at, min(chunk, nbins - at))
        local.append((coef_hbm.at[rows], coef.at[rows]))
    local.append((open_hbm.at[:, own_columns], open_own))
    local.append((closed_hbm.at[:, own_columns], closed_own))
    local.append((target_hbm.at[:, own_columns], target.at[0]))
    local = [
        pltpu.make_async_copy(source, held, local_sem.at[len(small) + i]) for i, (source, held) in enumerate(local)
    ]
    for copy in small + local:
        copy.start()
    for copy in small[:3]:
        copy.wait()

    bins[0, 0:4, :] = bins_ref[...].astype(F32)
    bins[0, 4:8, :] = rad_ref[...].astype(F32)
    sky[0, patches // 16 * 16 :, :] = jnp.zeros_like(sky[0, patches // 16 * 16 :, :])
    sky[0, 0:patches, :] = sky_in[...]

    for copy in small[3:]:
        copy.wait()
    area = area_ref[...]
    zone_row = lax.broadcasted_iota(jnp.int32, member.shape, 0)
    member[...] = jnp.where(zone_row == zone_ref[...], 1.0, 0.0).astype(BF16)

    def parts_of(value):
        first = value.astype(BF16).astype(F32)
        second = (value - first).astype(BF16).astype(F32)
        return first, second, value - first - second

    row = lax.broadcasted_iota(jnp.int32, (16, area.shape[1]), 0)
    stacked = jnp.zeros(row.shape, F32)
    for i, value in enumerate((area * openness_ref[...], area, area * area)):
        for part, rest in enumerate(parts_of(value)):
            stacked = jnp.where(row == 4 * part + i, rest, stacked)
    partial = lax.dot_general(
        stacked.astype(BF16), member[...], (((1,), (1,)), ((), ())), preferred_element_type=F32
    )
    stat_low[low, 0:4] = partial[0:4] + partial[4:8] + partial[8:12]
    stat_low[low, 4:8] = jnp.zeros((4, LANES), F32)

    lane = lax.broadcasted_iota(jnp.int32, (ROWS, LANES), 1).astype(F32)

    def build(d):
        columns[d * block : (d + 1) * block, :] = bins[d].T

        def rows_of(r, carry):
            at = pl.multiple_of(d * block + r * ROWS, ROWS)
            mine = columns[pl.ds(at, ROWS), :]
            place = [jnp.broadcast_to(mine[:, k : k + 1], (ROWS, LANES)) - lane for k in range(4)]
            value = [jnp.broadcast_to(mine[:, 4 + k : 5 + k], (ROWS, LANES)) for k in range(4)]
            for c in range(weights.shape[1] // LANES):
                first = float(c * LANES)
                w = jnp.zeros((ROWS, LANES), F32)
                for k in range(4):
                    w = jnp.where(place[k] == first, value[k], w)
                weights[pl.ds(at, ROWS), c * LANES : (c + 1) * LANES] = w.astype(BF16)
            return carry

        lax.fori_loop(0, block // ROWS, rows_of, 0)

    ends = 2 * (1 - lax.rem(lax.div(h + 1, 2), 2))
    pl.semaphore_wait(barrier, hours - 1 + SIDE - 1 + YS - 1 + ends)

    def remote(source, held, send, recv, device):
        return pltpu.make_async_remote_copy(
            src_ref=source, dst_ref=held, send_sem=send, recv_sem=recv, device_id=device, device_id_type=MESH
        )

    def spread(buffer, me, send, recv, device_of):
        mine = buffer.at[me]
        copies = [remote(mine, mine, send.at[d], recv.at[d], device_of(d)) for d in range(1, buffer.shape[0])]
        for copy in copies:
            copy.start()
        return copies

    def arrive(copies):
        for copy in copies:
            copy.wait_recv()

    def total_of(buffer):
        total = buffer[0]
        for m in range(1, buffer.shape[0]):
            total = total + buffer[m]
        return total

    stat_low_copies = spread(stat_low, low, low_send.at[0], low_recv.at[0], low_of)
    for d in range(1, YS):
        pl.semaphore_signal(y_ready, inc=1, device_id=y_of(d), device_id_type=MESH)
    bins_copies = []
    for d in range(1, hours):
        copy = remote(bins.at[0], bins.at[d], hour_send.at[0, d], hour_recv.at[0, d], hour_of(d))
        copy.start()
        bins_copies.append(copy)
    piece = pl.ds(pl.multiple_of(low * PIECE, PIECE), PIECE)
    sky_copies = []
    for d in range(1, hours):
        copy = remote(sky.at[0, piece], sky.at[d, piece], hour_send.at[1, d], hour_recv.at[1, d], hour_of(d))
        copy.start()
        sky_copies.append(copy)
    target_copies = []
    for d in range(1, hours):
        place = pl.ds(pl.multiple_of(lax.rem(h + d, hours) * own, own), own)
        copy = remote(target_hbm.at[:, place], target.at[d], hour_send.at[2, d], hour_recv.at[2, d], hour_of(d))
        copy.start()
        target_copies.append(copy)

    def sun_of(d):
        here = slice(d * block, (d + 1) * block)
        cross[d] = jnp.dot(weights[here, 0:whole], coef[0:whole, :], preferred_element_type=F32) + jnp.dot(
            weights[here, whole:], tail[...], preferred_element_type=F32
        )

    def levels_of(d):
        first = (((0,), (0,)), ((), ()))
        op_part = lax.dot_general(sky[d, 0:patches], open_own[...], first, preferred_element_type=F32)
        cl_part = lax.dot_general(sky[d, 0:patches], closed_own[...], first, preferred_element_type=F32)
        cross[d] = op_part - cl_part + cross[d]
        lit[d] = cl_part

    build(0)
    for copy in local:
        copy.wait()
    tail_wide[...] = jnp.zeros_like(tail_wide)
    tail_wide[0 : nbins - whole, :] = coef[whole:nbins, :].astype(F32)
    tail[...] = tail_wide[...].astype(BF16)
    sun_of(0)
    levels_of(0)

    arrive(stat_low_copies)
    group = half * YS + y
    stat_all[group] = total_of(stat_low)
    mine = stat_all.at[group]
    stat_y_copies = []
    for d in range(1, YS):
        copy = remote(mine, mine, y_send.at[d], y_recv.at[d], y_of(d))
        copy.start()
        stat_y_copies.append(copy)
    pl.semaphore_wait(y_ready, YS - 1)
    half_copies = [
        remote(mine, mine, half_send.at[t, there_y], half_recv.at[y], taker(t, there_y))
        for there_y in range(YS)
        for t in range(2)
    ]

    @pl.when(at_end)
    def _():
        for copy in half_copies:
            copy.start()

    arrive(sky_copies)
    sky_low_copies = []
    for d in range(1, SIDE):
        held = sky.at[1:, piece]
        copy = remote(held, held, low_send.at[1, d], low_recv.at[1, d], low_of(d))
        copy.start()
        sky_low_copies.append(copy)

    arrive(bins_copies)
    for d in range(1, hours):
        build(d)
    for d in range(1, hours):
        sun_of(d)
    arrive(sky_low_copies)
    for d in range(1, hours):
        levels_of(d)

    arrive(stat_y_copies)
    for there_y in range(YS):
        remote(mine, mine, half_send.at[0, 0], half_recv.at[there_y], taker(0, 0)).wait_recv()
    sums = total_of(stat_all)
    zone_lane = lax.broadcasted_iota(jnp.int32, (1, LANES), 1)
    den = jnp.where(zone_lane < 2 * PLANE, sums[1:2], 1.0)
    shares = sums[0:1] / den
    share = jnp.sum(jnp.where(zone_lane == s, shares, 0.0), axis=1, keepdims=True)

    lit_copies = []

    def send_lit(d, first, last, kind):
        rows = slice(first, last)
        copy = remote(
            lit_out.at[d, rows],
            lit_hbm.at[rows, own_columns],
            hour_send.at[kind, d],
            hour_recv.at[kind, d],
            hour_of(hours - d),
        )
        copy.start()
        lit_copies.append(copy)

    for d in range(hours):
        level = lit[d] + share * cross[d]
        lit[d] = level
        lit_out[d] = level.astype(BF16)
        if d:
            send_lit(d, 0, 16, 3)
    own_out = pltpu.make_async_copy(lit_out.at[0], lit_hbm.at[:, own_columns], local_sem.at[0])
    own_out.start()

    terms = jnp.zeros((1, own), F32)
    for d in range(hours):
        if d:
            target_copies[d - 1].wait_recv()
        part = 2.0 * (lit[d] - target[d].astype(F32)) * cross[d]
        terms = terms + jnp.sum(part, axis=0, keepdims=True)
    local_grad = jnp.sum(terms, axis=1, keepdims=True)
    grad_column[in_column] = jnp.where(zone_lane == s, local_grad, 0.0)
    column_copies = spread(grad_column, in_column, column_send, column_recv, column_of)
    for d in (1,):
        column_copies[d - 1].wait_recv()
    for d in range(1, hours):
        send_lit(d, 16, block, 4)
    arrive([column_copies[d - 1] for d in range(1, 2 * hours * CORES) if d not in (1,)])
    grad_all[chip] = total_of(grad_column)
    across_copies = spread(grad_all, chip, across_send, across_recv, across_of)
    arrive(across_copies)
    zone_grad = total_of(grad_all)
    ratio = zone_grad / den
    square = jnp.sum(ratio * ratio * sums[2:3], axis=1, keepdims=True)
    rms = jnp.sqrt(square / windows_all + 1e-06)
    first_part, second_part, third_part = parts_of(ratio)
    part_row = lax.broadcasted_iota(jnp.int32, (16, LANES), 0)
    parts = jnp.where(part_row == 0, first_part, jnp.where(part_row == 1, second_part, third_part))
    parts = jnp.where(part_row < 3, parts, 0.0).astype(BF16)
    chosen = jnp.dot(parts, member[...], preferred_element_type=F32)
    chosen = chosen[0:1] + chosen[1:2] + chosen[2:3]
    grad = area_ref[...] * chosen
    new_ref[...] = jnp.clip(openness_ref[...] - 0.25 * grad / rms, 0.0, 1.0)

    for copy in bins_copies + stat_low_copies + sky_copies + target_copies + stat_y_copies + sky_low_copies:
        copy.wait_send()
    for copy in column_copies + across_copies:
        copy.wait_send()

    @pl.when(at_end)
    def _():
        for copy in half_copies:
            copy.wait_send()

    own_out.wait()
    for copy in lit_copies:
        copy.wait()


def hand_over(lit_in, new_in, lit_hbm, new_hbm, sem):
    copies = [pltpu.make_async_copy(lit_in, lit_hbm, sem.at[0]), pltpu.make_async_copy(new_in, new_hbm, sem.at[1])]
    for copy in copies:
        copy.start()
    for copy in copies:
        copy.wait()


def solution(mesh):
    hours = mesh.shape["hour"]
    sens = mesh.shape["sens"]

    def step(sky, sky_open, sky_closed, sun_coef, sun_bins, sun_rad, target, zone_of, area, openness):
        block, patches = sky.shape
        nbins, own = sun_coef.shape
        windows = area.shape[0]
        padded = pl.cdiv(nbins, LANES) * LANES
        any_space = pl.BlockSpec(memory_space=pl.ANY)
        hbm = pl.BlockSpec(memory_space=pltpu.HBM)
        vmem = pl.BlockSpec(memory_space=pltpu.VMEM)
        tile = (SIDE, LANES)
        lit, new = pl.pallas_call(
            functools.partial(kernel, hours, windows * sens),
            out_shape=(
                jax.ShapeDtypeStruct((block, own * hours), BF16),
                jax.ShapeDtypeStruct((1, windows), F32),
            ),
            in_specs=[hbm] * 10,
            out_specs=(any_space, vmem),
            scratch_shapes=[
                pltpu.VMEM(sun_bins.T.shape, jnp.int32),
                pltpu.VMEM(sun_rad.T.shape, BF16),
                pltpu.VMEM((1, windows), jnp.int32),
                pltpu.VMEM((1, windows), F32),
                pltpu.VMEM((1, windows), F32),
                pltpu.VMEM((nbins, own), BF16),
                pltpu.VMEM((LANES, own), F32),
                pltpu.VMEM((LANES, own), BF16),
                pltpu.VMEM((hours * block, padded), BF16),
                pltpu.VMEM((hours * block, SIDE), F32),
                pltpu.VMEM((hours,) + tile, F32),
                pltpu.VMEM((patches, block), BF16),
                pltpu.VMEM((hours, SIDE * PIECE, block), BF16),
                pltpu.VMEM((hours, block, own), BF16),
                pltpu.VMEM((patches, own), BF16),
                pltpu.VMEM((patches, own), BF16),
                pltpu.VMEM((hours, block, own), F32),
                pltpu.VMEM((hours, block, own), F32),
                pltpu.VMEM((hours, block, own), BF16),
                pltpu.VMEM((LANES, windows), BF16),
                pltpu.VMEM((SIDE,) + tile, F32),
                pltpu.VMEM((2 * YS,) + tile, F32),
                pltpu.VMEM((2 * hours * CORES, 1, LANES), F32),
                pltpu.VMEM((PLANE // CORES, 1, LANES), F32),
                pltpu.SemaphoreType.DMA((16,)),
                pltpu.SemaphoreType.DMA((5, hours)),
                pltpu.SemaphoreType.DMA((5, hours)),
                pltpu.SemaphoreType.DMA((2, SIDE)),
                pltpu.SemaphoreType.DMA((2, SIDE)),
                pltpu.SemaphoreType.DMA((YS,)),
                pltpu.SemaphoreType.DMA((YS,)),
                pltpu.SemaphoreType.DMA((2, YS)),
                pltpu.SemaphoreType.DMA((YS,)),
                pltpu.SemaphoreType.DMA((2 * hours * CORES,)),
                pltpu.SemaphoreType.DMA((2 * hours * CORES,)),
                pltpu.SemaphoreType.DMA((PLANE // CORES,)),
                pltpu.SemaphoreType.DMA((PLANE // CORES,)),
                pltpu.SemaphoreType.REGULAR,
            ],
            compiler_params=pltpu.CompilerParams(
                collective_id=0, has_side_effects=True, vmem_limit_bytes=48 << 20
            ),
        )(
            *(
                pltpu.with_memory_space_constraint(x, pltpu.HBM)
                for x in (
                    sky.T,
                    sky_open,
                    sky_closed,
                    sun_coef,
                    sun_bins.T,
                    sun_rad.T,
                    target,
                    zone_of.T,
                    area[None, :],
                    openness[None, :],
                )
            )
        )
        lit, new = pl.pallas_call(
            hand_over,
            out_shape=(jax.ShapeDtypeStruct(lit.shape, BF16), jax.ShapeDtypeStruct(new.shape, F32)),
            in_specs=[vmem, vmem],
            out_specs=(any_space, any_space),
            scratch_shapes=[pltpu.SemaphoreType.DMA((2,))],
            compiler_params=pltpu.CompilerParams(vmem_limit_bytes=1 << 20),
        )(lit, new)
        return lit, new[0]

    in_specs = (
        P("hour", None),
        P(None, "sens"),
        P(None, "sens"),
        P(None, ("sens", "hour")),
        P("hour", None),
        P("hour", None),
        P("hour", "sens"),
        P("sens", None),
        P("sens"),
        P("sens"),
    )
    out_specs = (P("hour", "sens"), P("sens"))
    return jax.shard_map(step, mesh=mesh, in_specs=in_specs, out_specs=out_specs, check_vma=False)
```
